32 devices in a mesh: ctx: 8 (over z, y), head: 4 (over x, core).
Axes of the slice: x: 2, y: 2, z: 4, core: 2. Of those that a mesh axis runs over, the one named last changes fastest.
Arguments:
- inputs: bfloat16 [2048, 5376], P('ctx', 'head'), may hold values from -48 to 48
- positions: int32 [2048], P('ctx'), may hold values from 0 to 2047, as said below
- w_query: bfloat16 [5376, 4096], P(None, 'head'), may hold values from -0.125 to 0.125
- w_key: bfloat16 [5376, 2048], P(None, 'head'), may hold values from -0.125 to 0.125
- w_value: bfloat16 [5376, 2048], P(None, 'head'), may hold values from -0.078125 to 0.078125
- w_out: bfloat16 [4096, 5376], P('head'), may hold values from -1 to 1
- post_gain: bfloat16 [5376], P('head'), may hold values from 0.25 to 1.75
- cotangent: bfloat16 [2048, 5376], P('ctx', 'head'), may hold values from -6 to 6
Outputs:
- hidden: bfloat16 [2048, 5376], P('ctx', 'head')
- grad_inputs: bfloat16 [2048, 5376], P('ctx', 'head')
- grad_w_query: float32 [5376, 4096], P('ctx', 'head')
- grad_w_key: float32 [5376, 2048], P('ctx', 'head')
- grad_w_value: float32 [5376, 2048], P('ctx', 'head')
- grad_w_out: float32 [4096, 5376], P('head', 'ctx')
The draws below stay inside these ranges and needn't reach their ends.
Inputs may be any that keep to these rules, and one draw needn't show every extreme that they name: positions rise by one from each token to the next, except at the first token of a new document, where they are 0; the first token may lie in a document that began earlier.
All inputs are finite; a program needn't handle non-finite values.
Results may differ from the reference program's by a relative error of at most 0.02.
Values may be sent and summed in bfloat16 or wider, within the bound.
No kernel may reach another device: no remote copies, remote signals or barrier semaphores. Data moves between devices by JAX's collectives and lax.ppermute only.
A program may use at most 192 MiB of HBM per device.

```python
import math
import jax
import jax.numpy as jnp
from jax import lax

D = 5376
HEADS = 32
KV_HEADS = 16
HEAD_DIM = 128
WINDOW = 1024
TOK_DEV = 256
TOKENS = 2048
N_CTX = 8
N_HEAD = 4


def draw_inputs(key, part):
    base_key = jax.random.fold_in(key, 101)
    noise_part = jax.random.normal(jax.random.fold_in(base_key, 1), (TOKENS, D), jnp.float32)
    return jnp.clip(noise_part, -6.0, 6.0).astype(jnp.bfloat16)


def draw_positions(key, part):
    base_key = jax.random.fold_in(key, 505)
    offset = jax.random.randint(jax.random.fold_in(base_key, 1), (), 0, TOKENS)
    first_restart = TOKENS - offset
    room = jnp.maximum(TOKENS - first_restart, 1)
    later = first_restart + jax.random.randint(jax.random.fold_in(base_key, 2), (3,), 0, 1 << 30) % room
    restarts = jnp.concatenate([first_restart[None], later]).astype(jnp.int32)
    row_index = jnp.arange(TOKENS, dtype=jnp.int32)
    last_start = jnp.max(jnp.where(restarts[None, :] <= row_index[:, None], restarts[None, :], -offset), axis=1)
    return (row_index - last_start).astype(jnp.int32)


def query_base(key):
    base_key = jax.random.fold_in(key, 202)
    values = jax.random.normal(base_key, (D, HEADS * HEAD_DIM), jnp.float32)
    return values * D ** (-0.5)


def draw_w_query(key, part):
    return jnp.clip(query_base(key), -0.125, 0.125).astype(jnp.bfloat16)


def draw_w_key(key, part):
    own_part = jax.random.normal(jax.random.fold_in(key, 303), (D, KV_HEADS * HEAD_DIM), jnp.float32) * D ** (-0.5)
    return jnp.clip(own_part, -0.125, 0.125).astype(jnp.bfloat16)


def draw_w_out(key, part):
    base_key = jax.random.fold_in(key, 404)
    columns = jnp.arange(D, dtype=jnp.float32)[None, :] / (D - 1)
    values = jax.random.normal(base_key, (HEADS * HEAD_DIM, D), jnp.float32) * jnp.exp(math.log(10.0) * columns)
    return jnp.clip(values * (HEADS * HEAD_DIM) ** (-0.5), -1.0, 1.0).astype(jnp.bfloat16)


def level_of(own_key, shape, shards, least, largest):
    def one(axis_at, parts):
        steps = jax.random.uniform(jax.random.fold_in(jax.random.fold_in(own_key, 6), axis_at), (parts,), jnp.float32, least / len(shards), largest / len(shards))
        return jnp.repeat(jnp.exp(steps), shape[axis_at] // parts).reshape((-1,) + (1,) * (len(shape) - axis_at - 1))

    gain = one(*shards[0])
    for cut in shards[1:]:
        gain = gain * one(*cut)
    return gain


def bell_draw(rng, shape, deviation, most, cuts=(), kind=jnp.bfloat16):
    entries = jax.random.normal(rng, shape, jnp.float32) * deviation
    if len(cuts) > 0:
        entries = level_of(rng, shape, cuts, -0.22, 0.18) * entries
    return jnp.clip(entries, min=-most, max=most).astype(kind)


def setup_inputs(seed: int = 0) -> dict:
    streams_of = jax.random.split(jax.random.key(seed), 9)
    inputs = draw_inputs(jax.random.fold_in(streams_of[8], 71), 0)
    positions = draw_positions(jax.random.fold_in(streams_of[8], 71), 0)
    w_query = draw_w_query(jax.random.fold_in(streams_of[8], 71), 0)
    w_key = draw_w_key(jax.random.fold_in(streams_of[8], 71), 0)
    w_value = bell_draw(streams_of[4], (D, KV_HEADS * HEAD_DIM), D ** -0.5, 0.078125, ((1, 4),))
    w_out = draw_w_out(jax.random.fold_in(streams_of[8], 71), 0)
    post_gain = jnp.clip(1.0 + 0.15 * jax.random.normal(streams_of[6], (D,), jnp.float32), 0.25, 1.75).astype(jnp.bfloat16)
    cotangent = bell_draw(streams_of[7], (TOKENS, D), 1.0, 6.0, ((0, 8), (1, 4)))
    return {"inputs": inputs, "positions": positions, "w_query": w_query, "w_key": w_key, "w_value": w_value, "w_out": w_out, "post_gain": post_gain, "cotangent": cotangent}


EPSILON = 1e-06
ROPE_BASE = 10000.0

def rope_tables(positions, head_dim):
    half_dim = head_dim // 2
    frequency = jnp.exp(jnp.arange(half_dim, dtype=jnp.float32) * (-2.0 * math.log(ROPE_BASE) / head_dim))
    angles = positions.astype(jnp.float32)[:, None] * frequency[None, :]
    return (jnp.cos(angles)[:, None, :], jnp.sin(angles)[:, None, :])

def rotate(values, cosine, sine_table):
    half_dim = values.shape[-1] // 2
    first_half = values[..., :half_dim]
    second_half = values[..., half_dim:]
    return jnp.concatenate([first_half * cosine - second_half * sine_table, second_half * cosine + first_half * sine_table], axis=-1)

def window_mask(query_first, key_first, query_count, key_count, positions, window):
    query_index = query_first + jnp.arange(query_count, dtype=jnp.int32)
    key_index = key_first + jnp.arange(key_count, dtype=jnp.int32)
    distance = query_index[:, None] - key_index[None, :]
    return (key_index[None, :] >= 0) & (distance >= 0) & (distance < window) & (distance <= positions[:, None])

def widen(values):
    return lax.optimization_barrier(values).astype(jnp.float32)

def attend_forward(queries, key_block, value_block, allowed, score_scale):
    scores = jnp.einsum('tkgh,skh->kgts', widen(queries), widen(key_block)) * score_scale
    scores = jnp.where(allowed, scores, -jnp.inf)
    highest = lax.optimization_barrier(jnp.max(scores, axis=-1, keepdims=True))
    exponent = jnp.exp(scores - highest)
    probability = exponent / lax.optimization_barrier(jnp.sum(exponent, axis=-1, keepdims=True))
    weights = probability.astype(jnp.bfloat16)
    attended = jnp.einsum('kgts,skh->tkgh', widen(weights), widen(value_block)).astype(jnp.bfloat16)
    return (probability, weights, attended)

def attend_backward(queries, key_block, value_block, probability, weights, grad_attended, score_scale):
    grad_weights = jnp.einsum('tkgh,skh->kgts', widen(grad_attended), widen(value_block))
    inner = lax.optimization_barrier(jnp.sum(probability * grad_weights, axis=-1, keepdims=True))
    grad_scores = (probability * (grad_weights - inner)).astype(jnp.bfloat16)
    grad_query_part = jnp.einsum('kgts,skh->tkgh', widen(grad_scores), widen(key_block)) * score_scale
    grad_key_part = jnp.einsum('kgts,tkgh->skh', widen(grad_scores), widen(queries)) * score_scale
    grad_value_part = jnp.einsum('kgts,tkgh->skh', widen(weights), widen(grad_attended))
    return (grad_query_part, grad_key_part, grad_value_part)

def reference(inputs, positions, w_query, w_key, w_value, w_out, post_gain, cotangent):
    total_rows = inputs.shape[0]
    group_size = HEADS // KV_HEADS
    score_scale = (D // HEADS) ** (-0.5)
    span_rows = WINDOW + TOK_DEV
    cosine, sine_table = rope_tables(positions, HEAD_DIM)
    queries = rotate(jnp.dot(inputs, w_query, preferred_element_type=jnp.float32).reshape(total_rows, HEADS, HEAD_DIM), cosine, sine_table).astype(jnp.bfloat16)
    keys_all = rotate(jnp.dot(inputs, w_key, preferred_element_type=jnp.float32).reshape(total_rows, KV_HEADS, HEAD_DIM), cosine, sine_table).astype(jnp.bfloat16)
    values_all = jnp.dot(inputs, w_value, preferred_element_type=jnp.float32).astype(jnp.bfloat16).reshape(total_rows, KV_HEADS, HEAD_DIM)
    grouped = queries.reshape(total_rows, KV_HEADS, group_size, HEAD_DIM)
    padding = jnp.zeros((WINDOW, KV_HEADS, HEAD_DIM), jnp.bfloat16)
    padded_keys = jnp.concatenate([padding, keys_all], axis=0)
    padded_values = jnp.concatenate([padding, values_all], axis=0)
    blocks = jnp.arange(N_CTX, dtype=jnp.int32)

    def block_inputs(block):
        query_first = block * TOK_DEV
        block_queries = lax.dynamic_slice_in_dim(grouped, query_first, TOK_DEV, 0)
        key_block = lax.dynamic_slice_in_dim(padded_keys, query_first, span_rows, 0)
        value_block = lax.dynamic_slice_in_dim(padded_values, query_first, span_rows, 0)
        block_positions = lax.dynamic_slice_in_dim(positions, query_first, TOK_DEV, 0)
        allowed = window_mask(query_first, query_first - WINDOW, TOK_DEV, span_rows, block_positions, WINDOW)
        return (block_queries, key_block, value_block, allowed)

    def forward_block(block):
        block_queries, key_block, value_block, allowed = block_inputs(block)
        probability, weights, attended = attend_forward(block_queries, key_block, value_block, allowed, score_scale)
        return attended
    attended = lax.map(forward_block, blocks).reshape(total_rows, HEADS * HEAD_DIM)
    query_cols = HEADS * HEAD_DIM // N_HEAD
    key_cols = KV_HEADS * HEAD_DIM // N_HEAD
    branch = jnp.zeros((total_rows, D), jnp.float32)
    for head_group in range(N_HEAD):
        lower = head_group * query_cols
        partial_value = jnp.dot(attended[:, lower:lower + query_cols], w_out[lower:lower + query_cols], preferred_element_type=jnp.float32).astype(jnp.bfloat16)
        branch = branch + widen(partial_value)
    inverse_norm = lax.rsqrt(lax.optimization_barrier(jnp.sum(branch * branch, axis=1)) / D + EPSILON)
    normed = branch * inverse_norm[:, None]
    gain_all = post_gain.astype(jnp.float32)
    hidden = (inputs.astype(jnp.float32) + normed * gain_all[None, :]).astype(jnp.bfloat16)
    scaled_grad = cotangent.astype(jnp.float32) * gain_all[None, :]
    slopes = lax.optimization_barrier(jnp.sum(scaled_grad * normed, axis=1))
    branch_grad = (inverse_norm[:, None] * (scaled_grad - normed * (slopes / D)[:, None])).astype(jnp.bfloat16)
    grad_attended = jnp.dot(branch_grad, w_out.T, preferred_element_type=jnp.float32).astype(jnp.bfloat16)
    grad_w_out = jnp.dot(attended.T, branch_grad, preferred_element_type=jnp.float32)
    grad_grouped = grad_attended.reshape(total_rows, KV_HEADS, group_size, HEAD_DIM)

    def backward_block(sums, block):
        block_queries, key_block, value_block, allowed = block_inputs(block)
        probability, weights, attended_unused = attend_forward(block_queries, key_block, value_block, allowed, score_scale)
        block_grads = lax.dynamic_slice_in_dim(grad_grouped, block * TOK_DEV, TOK_DEV, 0)
        grad_query_part, grad_key_part, grad_value_part = attend_backward(block_queries, key_block, value_block, probability, weights, block_grads, score_scale)
        current = lax.dynamic_slice_in_dim(sums, block * TOK_DEV, span_rows, 1)
        sums = lax.dynamic_update_slice_in_dim(sums, current + jnp.stack([grad_key_part, grad_value_part]), block * TOK_DEV, 1)
        return (sums, grad_query_part)
    start_sums = jnp.zeros((2, WINDOW + total_rows, KV_HEADS, HEAD_DIM), jnp.float32)
    sums, query_grad_blocks = lax.scan(backward_block, start_sums, blocks)
    grad_key_rows = rotate(sums[0, WINDOW:], cosine, -sine_table).astype(jnp.bfloat16).reshape(total_rows, KV_HEADS * HEAD_DIM)
    grad_value_rows = sums[1, WINDOW:].astype(jnp.bfloat16).reshape(total_rows, KV_HEADS * HEAD_DIM)
    grad_query_rows = rotate(query_grad_blocks.reshape(total_rows, HEADS, HEAD_DIM), cosine, -sine_table).astype(jnp.bfloat16).reshape(total_rows, HEADS * HEAD_DIM)
    input_sum = jnp.zeros((total_rows, D), jnp.float32)
    for head_group in range(N_HEAD):
        query_low = head_group * query_cols
        key_low = head_group * key_cols
        term = jnp.dot(grad_query_rows[:, query_low:query_low + query_cols], w_query[:, query_low:query_low + query_cols].T, preferred_element_type=jnp.float32)
        term = term + jnp.dot(grad_key_rows[:, key_low:key_low + key_cols], w_key[:, key_low:key_low + key_cols].T, preferred_element_type=jnp.float32)
        term = term + jnp.dot(grad_value_rows[:, key_low:key_low + key_cols], w_value[:, key_low:key_low + key_cols].T, preferred_element_type=jnp.float32)
        input_sum = input_sum + widen(term.astype(jnp.bfloat16))
    grad_inputs = (cotangent.astype(jnp.float32) + input_sum).astype(jnp.bfloat16)
    grad_w_query = jnp.dot(inputs.T, grad_query_rows, preferred_element_type=jnp.float32)
    grad_w_key = jnp.dot(inputs.T, grad_key_rows, preferred_element_type=jnp.float32)
    grad_w_value = jnp.dot(inputs.T, grad_value_rows, preferred_element_type=jnp.float32)
    return (hidden, grad_inputs, grad_w_query, grad_w_key, grad_w_value, grad_w_out)
```

```python
import functools
import math

import jax
import jax.numpy as jnp
from jax import lax
from jax.experimental import pallas as pl
from jax.experimental.pallas import tpu as pltpu
from jax.sharding import PartitionSpec as P

D = 5376
HEADS = 32
HEAD_DIM = 128
WINDOW = 1024
EPSILON = 1e-06
ROPE_BASE = 10000.0
MASKED = -1e30


F32 = jnp.float32
BF16 = jnp.bfloat16


def send(value, axis, target):
    count = lax.axis_size(axis)
    pairs = [(i, target(i)) for i in range(count) if 0 <= target(i) < count]
    return lax.ppermute(value, axis, pairs)


def flip(value, axis, bit):
    return send(value, axis, lambda i: i ^ bit)


def gather_relative(value):
    pieces = [value]
    for j in range(1, lax.axis_size("head")):
        low = j & -j
        pieces.append(flip(pieces[j ^ low], "head", low))
    return pieces


def natural(pieces, head):
    bit = 1
    while bit < len(pieces):
        swap = (head & bit) != 0
        pieces = [jnp.where(swap, pieces[q ^ bit], pieces[q]) for q in range(len(pieces))]
        bit *= 2
    return pieces


def reduce_relative(keep, out):
    received = flip(out, "head", 1)
    sums = [keep[k].astype(F32) + received[k].astype(F32) for k in range(keep.shape[0])]
    bit = 2
    while len(sums) > 1:
        moved = flip(jnp.stack(sums[1::2]).astype(BF16), "head", bit)
        sums = [s + moved[k].astype(F32) for k, s in enumerate(sums[0::2])]
        bit *= 2
    return sums[0]


def gather_context(value):
    count = lax.axis_size("ctx")
    own = [value]
    for _ in range(count // 2 - 1):
        own.append(send(own[-1], "ctx", lambda i: (i + 2) % count))
    return own, [flip(v, "ctx", 1) for v in own]


def exchange_columns(chunks, ctx, head):
    count = lax.axis_size("ctx")
    depth = count // 2
    column, row = ctx % 2, ctx // 2

    def chunk(s):
        return lax.dynamic_index_in_dim(chunks, (row + s) % depth, 0, keepdims=False)

    arrived = [chunk(0)]
    for s in range(1, depth):
        arrived.append(send(chunk(s), "ctx", lambda i, s=s: (i + 2 * s) % count))
    arrived = jnp.stack(arrived)
    width = arrived.shape[2] // 2
    first, second = arrived[:, :, :width], arrived[:, :, width:]
    mine = jnp.where(column == 0, first, second)
    other = flip(jnp.where(column == 0, second, first), "ctx", 1)
    both = jnp.stack([mine, other])
    rows = natural(gather_relative(both), head)
    return [
        [jnp.concatenate([r[side, s] for r in rows], axis=0) for s in range(depth)]
        for side in range(2)
    ]


def split_columns(rows, parts):
    width = rows.shape[1] // parts
    return jnp.stack([rows[:, q * width : (q + 1) * width] for q in range(parts)])


def params(**kw):
    return pltpu.CompilerParams(vmem_limit_bytes=60 * 1024 * 1024, **kw)


def whole(shape):
    return pl.BlockSpec(shape, lambda *_: (0,) * len(shape))


def cost(flops, nbytes, transcendentals=0):
    return pl.CostEstimate(flops=flops, bytes_accessed=nbytes, transcendentals=transcendentals)


def turned(values, cos2, sin2):
    return values * cos2 + pltpu.roll(values, HEAD_DIM // 2, 1) * sin2


def multiply_pieces(head, pieces, w_ref):
    total = None
    depth = pieces[0].shape[1]
    for j, piece in enumerate(pieces):
        start = pl.multiple_of((head ^ j) * depth, 16)
        term = jnp.dot(piece[...], w_ref[pl.ds(start, depth), :], preferred_element_type=F32)
        total = term if total is None else total + term
    return total


def store_turned(out_ref, total, cos_ref, sin_ref, lead):
    for c in range(total.shape[1] // HEAD_DIM):
        cols = slice(c * HEAD_DIM, (c + 1) * HEAD_DIM)
        out_ref[lead + (slice(None), cols)] = turned(
            total[:, cols], cos_ref[...], sin_ref[...]
        ).astype(out_ref.dtype)


def query_kernel(count, head_ref, *refs):
    pieces, (w_ref, cos_ref, sin_ref, out_ref) = refs[:count], refs[count:]
    total = multiply_pieces(head_ref[0], pieces, w_ref)
    store_turned(out_ref, total, cos_ref, sin_ref, ())


def project_queries(head, pieces, weight, cos2, sin2):
    rows, depth = pieces[0].shape
    cols = weight.shape[1]
    block = min(256, cols)
    grid_spec = pltpu.PrefetchScalarGridSpec(
        num_scalar_prefetch=1,
        grid=(cols // block,),
        in_specs=[whole((rows, depth))] * len(pieces)
        + [pl.BlockSpec((weight.shape[0], block), lambda i, h: (0, i))]
        + [whole((rows, HEAD_DIM))] * 2,
        out_specs=pl.BlockSpec((rows, block), lambda i, h: (0, i)),
    )
    return pl.pallas_call(
        functools.partial(query_kernel, len(pieces)),
        grid_spec=grid_spec,
        out_shape=jax.ShapeDtypeStruct((rows, cols), BF16),
        compiler_params=params(),
        cost_estimate=cost(2 * rows * weight.size, 2 * weight.size),
        name="project_queries",
    )(head, *pieces, weight, cos2, sin2)


def pair_kernel(count, steps, head_ref, *refs):
    pieces, (k_ref, v_ref, cos_ref, sin_ref, out_ref) = refs[:count], refs[count:]

    @pl.when(pl.program_id(0) < steps)
    def _():
        total = multiply_pieces(head_ref[0], pieces, k_ref)
        store_turned(out_ref, total, cos_ref, sin_ref, (0,))

    @pl.when(pl.program_id(0) >= steps)
    def _():
        total = multiply_pieces(head_ref[0], pieces, v_ref)
        out_ref[0] = total.astype(out_ref.dtype)


def project_pair(head, pieces, w_key, w_value, cos2, sin2):
    rows, depth = pieces[0].shape
    cols = w_key.shape[1]
    block = min(256, cols)
    steps = cols // block
    grid_spec = pltpu.PrefetchScalarGridSpec(
        num_scalar_prefetch=1,
        grid=(2 * steps,),
        in_specs=[whole((rows, depth))] * len(pieces)
        + [
            pl.BlockSpec((w_key.shape[0], block), lambda i, h: (0, jnp.minimum(i, steps - 1))),
            pl.BlockSpec((w_key.shape[0], block), lambda i, h: (0, jnp.maximum(i - steps, 0))),
        ]
        + [whole((rows, HEAD_DIM))] * 2,
        out_specs=pl.BlockSpec((1, rows, block), lambda i, h: (i // steps, 0, i % steps)),
    )
    return pl.pallas_call(
        functools.partial(pair_kernel, len(pieces), steps),
        grid_spec=grid_spec,
        out_shape=jax.ShapeDtypeStruct((2, rows, cols), BF16),
        compiler_params=params(),
        cost_estimate=cost(4 * rows * w_key.size, 4 * w_key.size),
        name="project_pair",
    )(head, *pieces, w_key, w_value, cos2, sin2)


def fill_bias(bias_ref, ctx, pos_ref):
    spans, rows, _ = bias_ref.shape
    for d in range(spans):
        key = lax.broadcasted_iota(jnp.int32, (rows, rows), 0)
        query = lax.broadcasted_iota(jnp.int32, (rows, rows), 1)
        distance = d * rows + query - key
        reach = jnp.where(ctx >= d, pos_ref[...], -1)
        allowed = (distance >= 0) & (distance < WINDOW) & (distance <= reach)
        bias_ref[d] = jnp.where(allowed, 0.0, MASKED)


def head_rows(ref, group):
    return jnp.concatenate(
        [ref[:, g * HEAD_DIM : (g + 1) * HEAD_DIM] for g in range(group)], axis=0
    )


def dot_on(left, right, left_dim, right_dim):
    return lax.dot_general(
        left, right, (((left_dim,), (right_dim,)), ((), ())), preferred_element_type=F32
    )


def forward_kernel(spans, group, scale, ctx_ref, pos_ref, q_ref, *refs):
    pairs, (out_ref, lse_ref, bias_ref, score_ref) = refs[:spans], refs[spans:]

    @pl.when(pl.program_id(0) == 0)
    def _():
        fill_bias(bias_ref, ctx_ref[0], pos_ref)

    queries = head_rows(q_ref, group)
    highest = None
    for d in range(spans):
        scores = dot_on(pairs[d][0], queries, 1, 1) * scale
        scores = scores + jnp.concatenate([bias_ref[d]] * group, axis=1)
        score_ref[d] = scores
        top = jnp.max(scores, axis=0, keepdims=True)
        highest = top if highest is None else jnp.maximum(highest, top)
    total = None
    for d in range(spans):
        exponent = jnp.exp(score_ref[d] - highest)
        score_ref[d] = exponent
        part = jnp.sum(exponent, axis=0, keepdims=True)
        total = part if total is None else total + part
    inverse = 1.0 / total
    mixed = None
    for d in range(spans):
        weights = (score_ref[d] * inverse).astype(BF16)
        part = dot_on(pairs[d][1], weights, 0, 0)
        mixed = part if mixed is None else mixed + part
    rows = mixed.T
    count = q_ref.shape[0]
    for g in range(group):
        out_ref[:, g * HEAD_DIM : (g + 1) * HEAD_DIM] = rows[
            g * count : (g + 1) * count
        ].astype(BF16)
    lse_ref[0] = highest + jnp.log(total)


def attend_forward(ctx, positions, queries, pairs, group, scale):
    rows, cols = queries.shape
    spans = len(pairs)
    kv = cols // (group * HEAD_DIM)
    wide = group * HEAD_DIM
    grid_spec = pltpu.PrefetchScalarGridSpec(
        num_scalar_prefetch=1,
        grid=(kv,),
        in_specs=[whole((1, rows)), pl.BlockSpec((rows, wide), lambda g, c: (0, g))]
        + [pl.BlockSpec((2, rows, HEAD_DIM), lambda g, c: (0, 0, g))] * spans,
        out_specs=[
            pl.BlockSpec((rows, wide), lambda g, c: (0, g)),
            pl.BlockSpec((1, 1, group * rows), lambda g, c: (g, 0, 0)),
        ],
        scratch_shapes=[
            pltpu.VMEM((spans, rows, rows), F32),
            pltpu.VMEM((spans, rows, group * rows), F32),
        ],
    )
    area = spans * rows * rows * kv * group
    return pl.pallas_call(
        functools.partial(forward_kernel, spans, group, scale),
        grid_spec=grid_spec,
        out_shape=[
            jax.ShapeDtypeStruct((rows, cols), BF16),
            jax.ShapeDtypeStruct((kv, 1, group * rows), F32),
        ],
        compiler_params=params(),
        cost_estimate=cost(4 * area * HEAD_DIM, 8 * rows * cols, area),
        name="attend_forward",
    )(ctx, positions, queries, *pairs)


def backward_kernel(spans, group, scale, ctx_ref, pos_ref, q_ref, g_ref, lse_ref, *refs):
    cos_ref, sin_ref = refs[:2]
    pairs = refs[2 : 2 + spans]
    dq_ref = refs[2 + spans]
    outs = refs[3 + spans : 3 + 2 * spans]
    bias_ref, prob_ref, slope_ref = refs[3 + 2 * spans :]

    @pl.when(pl.program_id(0) == 0)
    def _():
        fill_bias(bias_ref, ctx_ref[0], pos_ref)

    queries = head_rows(q_ref, group)
    grads = head_rows(g_ref, group)
    lse = lse_ref[0]
    inner = None
    for d in range(spans):
        scores = dot_on(pairs[d][0], queries, 1, 1) * scale
        scores = scores + jnp.concatenate([bias_ref[d]] * group, axis=1)
        probability = jnp.exp(scores - lse)
        slope = dot_on(pairs[d][1], grads, 1, 1)
        prob_ref[d] = probability
        slope_ref[d] = slope
        part = jnp.sum(probability * slope, axis=0, keepdims=True)
        inner = part if inner is None else inner + part
    total = None
    for d in range(spans):
        probability = prob_ref[d]
        outs[d][1] = jnp.dot(
            probability.astype(BF16), grads, preferred_element_type=F32
        ).astype(outs[d].dtype)
        change = (probability * (slope_ref[d] - inner)).astype(BF16)
        outs[d][0] = (jnp.dot(change, queries, preferred_element_type=F32) * scale).astype(
            outs[d].dtype
        )
        part = dot_on(pairs[d][0], change, 0, 0)
        total = part if total is None else total + part
    rows = (total * scale).T
    count = q_ref.shape[0]
    for g in range(group):
        dq_ref[:, g * HEAD_DIM : (g + 1) * HEAD_DIM] = turned(
            rows[g * count : (g + 1) * count], cos_ref[...], -sin_ref[...]
        ).astype(BF16)


def attend_backward(ctx, positions, queries, grads, lse, cos2, sin2, pairs, group, scale):
    rows, cols = queries.shape
    spans = len(pairs)
    kv = cols // (group * HEAD_DIM)
    wide = group * HEAD_DIM
    pair_spec = pl.BlockSpec((2, rows, HEAD_DIM), lambda g, c: (0, 0, g))
    row_spec = pl.BlockSpec((rows, wide), lambda g, c: (0, g))
    grid_spec = pltpu.PrefetchScalarGridSpec(
        num_scalar_prefetch=1,
        grid=(kv,),
        in_specs=[
            whole((1, rows)),
            row_spec,
            row_spec,
            pl.BlockSpec((1, 1, group * rows), lambda g, c: (g, 0, 0)),
            whole((rows, HEAD_DIM)),
            whole((rows, HEAD_DIM)),
        ]
        + [pair_spec] * spans,
        out_specs=[row_spec] + [pair_spec] * spans,
        scratch_shapes=[
            pltpu.VMEM((spans, rows, rows), F32),
            pltpu.VMEM((spans, rows, group * rows), F32),
            pltpu.VMEM((spans, rows, group * rows), F32),
        ],
    )
    area = spans * rows * rows * kv * group
    shape = (2, rows, kv * HEAD_DIM)
    return pl.pallas_call(
        functools.partial(backward_kernel, spans, group, scale),
        grid_spec=grid_spec,
        out_shape=[jax.ShapeDtypeStruct((rows, cols), BF16), jax.ShapeDtypeStruct(shape, F32)]
        + [jax.ShapeDtypeStruct(shape, BF16)] * (spans - 1),
        compiler_params=params(),
        cost_estimate=cost(10 * area * HEAD_DIM, 16 * rows * cols, area),
        name="attend_backward",
    )(ctx, positions, queries, grads, lse, cos2, sin2, *pairs)


def branch_kernel(count, head_ref, a_ref, w_ref, keep_ref, out_ref):
    rows = a_ref.shape[0] // count
    order = list(range(0, count, 2)) + list(range(1, count, 2))
    left = jnp.concatenate(
        [a_ref[pl.ds(pl.multiple_of((head_ref[0] ^ j) * rows, 16), rows), :] for j in order],
        axis=0,
    )
    total = jnp.dot(left, w_ref[...], preferred_element_type=F32).astype(BF16)
    half = count // 2
    for k in range(half):
        keep_ref[k] = total[k * rows : (k + 1) * rows]
        out_ref[k] = total[(half + k) * rows : (half + k + 1) * rows]


def project_branch(head, attended, w_out, count):
    rows, depth = attended.shape
    cols = w_out.shape[1]
    block = cols // 7 if cols % (7 * 128) == 0 else 128
    shape = jax.ShapeDtypeStruct((count // 2, rows // count, cols), BF16)
    spec = pl.BlockSpec((count // 2, rows // count, block), lambda i, h: (0, 0, i))
    grid_spec = pltpu.PrefetchScalarGridSpec(
        num_scalar_prefetch=1,
        grid=(cols // block,),
        in_specs=[whole((rows, depth)), pl.BlockSpec((depth, block), lambda i, h: (0, i))],
        out_specs=[spec, spec],
    )
    return pl.pallas_call(
        functools.partial(branch_kernel, count),
        grid_spec=grid_spec,
        out_shape=[shape, shape],
        compiler_params=params(),
        cost_estimate=cost(2 * rows * w_out.size, 2 * w_out.size),
        name="project_branch",
    )(head, attended, w_out)


def attended_grad_kernel(count, head_ref, *refs):
    pieces, (w_ref, out_ref, rows_ref) = refs[:count], refs[count:]
    rows = pieces[0].shape[0]

    @pl.when(pl.program_id(0) == 0)
    def _():
        for j, piece in enumerate(pieces):
            start = pl.multiple_of((head_ref[0] ^ j) * rows, 16)
            rows_ref[pl.ds(start, rows), :] = piece[...]

    out_ref[...] = dot_on(rows_ref[...], w_ref[...], 1, 1).astype(BF16)


def attended_grad(head, pieces, w_out):
    rows, cols = pieces[0].shape
    count = len(pieces)
    block = min(256, w_out.shape[0])
    grid_spec = pltpu.PrefetchScalarGridSpec(
        num_scalar_prefetch=1,
        grid=(w_out.shape[0] // block,),
        in_specs=[whole((rows, cols))] * count
        + [pl.BlockSpec((block, cols), lambda i, h: (i, 0))],
        out_specs=pl.BlockSpec((rows * count, block), lambda i, h: (0, i)),
        scratch_shapes=[pltpu.VMEM((rows * count, cols), BF16)],
    )
    return pl.pallas_call(
        functools.partial(attended_grad_kernel, count),
        grid_spec=grid_spec,
        out_shape=jax.ShapeDtypeStruct((rows * count, w_out.shape[0]), BF16),
        compiler_params=params(),
        cost_estimate=cost(2 * rows * count * w_out.size, 2 * w_out.size),
        name="attended_grad",
    )(head, *pieces, w_out)


def inputs_grad_kernel(head_ref, q_ref, k_ref, v_ref, wq_ref, wk_ref, wv_ref, out_ref):
    total = dot_on(q_ref[...], wq_ref[...], 1, 1)
    total = total + dot_on(k_ref[...], wk_ref[...], 1, 1)
    total = total + dot_on(v_ref[...], wv_ref[...], 1, 1)
    out_ref[0] = total.astype(BF16)


def inputs_grad(head, parity, count, dq, dk, dv, w_query, w_key, w_value):
    rows = dq.shape[0]
    depth = w_query.shape[0] // count

    def weight_spec(weight):
        return pl.BlockSpec((depth, weight.shape[1]), lambda i, h: (h[0] ^ (2 * i + parity), 0))

    grid_spec = pltpu.PrefetchScalarGridSpec(
        num_scalar_prefetch=1,
        grid=(count // 2,),
        in_specs=[whole(dq.shape), whole(dk.shape), whole(dv.shape)]
        + [weight_spec(w) for w in (w_query, w_key, w_value)],
        out_specs=pl.BlockSpec((1, rows, depth), lambda i, h: (i, 0, 0)),
    )
    size = (w_query.size + 2 * w_key.size) // 2
    return pl.pallas_call(
        inputs_grad_kernel,
        grid_spec=grid_spec,
        out_shape=jax.ShapeDtypeStruct((count // 2, rows, depth), BF16),
        compiler_params=params(),
        cost_estimate=cost(2 * rows * size, 2 * size),
        name="inputs_grad",
    )(head, dq, dk, dv, w_query, w_key, w_value)


def contract_first(left_side, right_side):
    return dot_on(left_side, right_side, 0, 0)


def weight_grad(lefts, rights):
    total = None
    for left, right in zip(lefts[0] + lefts[1], rights[0] + rights[1], strict=True):
        term = contract_first(left, right)
        total = term if total is None else total + term
    return total


def local(inputs, positions, w_query, w_key, w_value, w_out, post_gain, cotangent):
    tok_rows, part_cols = inputs.shape
    n_ctx, n_head = lax.axis_size("ctx"), lax.axis_size("head")
    kv_cols = w_key.shape[1]
    group = w_query.shape[1] // kv_cols
    halo = WINDOW // tok_rows
    own_rows = tok_rows // n_head
    scale = (D // HEADS) ** (-0.5)
    ctx, head = lax.axis_index("ctx"), lax.axis_index("head")
    ctx_arg, head_arg = ctx.reshape(1), head.reshape(1)
    column = ctx % 2
    half = HEAD_DIM // 2
    frequency = jnp.exp(jnp.arange(half, dtype=F32) * (-2.0 * math.log(ROPE_BASE) / HEAD_DIM))
    angles = positions.astype(F32)[:, None] * frequency[None, :]
    cosine, sine = jnp.cos(angles), jnp.sin(angles)
    cos2 = jnp.concatenate([cosine, cosine], axis=1)
    sin2 = jnp.concatenate([-sine, sine], axis=1)
    pos_row = positions.reshape(1, tok_rows)

    pieces = gather_relative(inputs)
    pair = project_pair(head_arg, pieces, w_key, w_value, cos2, sin2)
    own_chain = [pair]
    crossed = []
    for i in range(halo // 2):
        own_chain.append(send(own_chain[-1], "ctx", lambda i: i + 2))
        crossed.append(flip(jnp.where(column == 0, own_chain[i], own_chain[i + 1]), "ctx", 1))
    pairs = [pair]
    for i in range(halo // 2):
        pairs += [crossed[i], own_chain[i + 1]]
    queries = project_queries(head_arg, pieces, w_query, cos2, sin2)

    input_parts = natural(
        [lax.dynamic_slice_in_dim(p, head * own_rows, own_rows, 0) for p in pieces], head
    )
    bundles = []
    for j in range(n_head):
        rows = lax.dynamic_slice_in_dim(cotangent, (head ^ j) * own_rows, own_rows, 0)
        bundle = jnp.concatenate([rows, post_gain[None, :]], axis=0)
        bundles.append(flip(bundle, "head", j) if j else bundle)
    bundle_rows = jnp.concatenate(natural(bundles, head), axis=1).astype(F32)
    cotangent_rows, gain = bundle_rows[:own_rows], bundle_rows[own_rows:]
    input_rows = jnp.concatenate(input_parts, axis=1)

    attended, lse = attend_forward(ctx_arg, pos_row, queries, pairs, group, scale)
    keep, out = project_branch(head_arg, attended, w_out, n_head)
    branch = reduce_relative(keep, out)
    inverse_norm = lax.rsqrt(jnp.sum(branch * branch, axis=1, keepdims=True) / D + EPSILON)
    normed = branch * inverse_norm
    hidden_rows = (input_rows.astype(F32) + normed * gain).astype(BF16)
    scaled_grad = cotangent_rows * gain
    slopes = jnp.sum(scaled_grad * normed, axis=1, keepdims=True)
    branch_grad = (inverse_norm * (scaled_grad - normed * (slopes / D))).astype(BF16)
    grad_attended = attended_grad(head_arg, gather_relative(branch_grad), w_out)

    attended_all = gather_context(attended)
    depth = n_ctx // 2
    if depth == n_head:
        input_chunks = jnp.stack(input_parts)
    else:
        input_chunks = split_columns(input_rows, depth)
    input_cols = exchange_columns(input_chunks, ctx, head)

    grads = attend_backward(
        ctx_arg, pos_row, queries, grad_attended, lse, cos2, sin2, pairs, group, scale
    )
    grad_query_rows, parts = grads[0], grads[1:]
    crossing = [flip(parts[d], "ctx", 1) for d in range(1, halo + 1, 2)]
    carried = None
    for i in range(halo // 2, -1, -1):
        slot = parts[2 * i].astype(F32)
        here = crossing[i].astype(F32) if i < halo // 2 else 0.0
        there = crossing[i - 1].astype(F32) if i > 0 else 0.0
        slot = slot + jnp.where(column == 0, here, there)
        if carried is not None:
            slot = slot + carried.astype(F32)
        if i > 0:
            carried = send(slot.astype(BF16), "ctx", lambda i: i - 2)
    heads_shape = (tok_rows, kv_cols // HEAD_DIM, HEAD_DIM)
    key_sum = slot[0].reshape(heads_shape)
    first, second = key_sum[..., :half], key_sum[..., half:]
    cos3, sin3 = cosine[:, None, :], sine[:, None, :]
    grad_key_rows = jnp.concatenate(
        [first * cos3 + second * sin3, second * cos3 - first * sin3], axis=-1
    )
    grad_key_rows = grad_key_rows.reshape(tok_rows, kv_cols).astype(BF16)
    grad_value_rows = slot[1].astype(BF16)

    query_all = gather_context(grad_query_rows)
    pair_all = gather_context(jnp.concatenate([grad_key_rows, grad_value_rows], axis=1))
    grad_cols = exchange_columns(split_columns(branch_grad, depth), ctx, head)
    grad_w_out = weight_grad(attended_all, grad_cols)

    moved = [
        inputs_grad(
            head_arg, parity, n_head, grad_query_rows, grad_key_rows, grad_value_rows,
            w_query, w_key, w_value,
        )
        for parity in (1, 0)
    ]
    grad_inputs = (cotangent.astype(F32) + reduce_relative(moved[1], moved[0])).astype(BF16)
    grad_w_query = weight_grad(input_cols, query_all)
    grad_w_pair = weight_grad(input_cols, pair_all)

    hidden_chunks = split_columns(hidden_rows, n_head)
    hidden_parts = []
    for j in range(n_head):
        chunk = lax.dynamic_index_in_dim(hidden_chunks, head ^ j, 0, keepdims=False)
        hidden_parts.append(flip(chunk, "head", j) if j else chunk)
    hidden = jnp.concatenate(natural(hidden_parts, head), axis=0)
    return (
        hidden,
        grad_inputs,
        grad_w_query,
        grad_w_pair[:, :kv_cols],
        grad_w_pair[:, kv_cols:],
        grad_w_out,
    )


def solution(mesh):
    in_specs = (
        P("ctx", "head"),
        P("ctx"),
        P(None, "head"),
        P(None, "head"),
        P(None, "head"),
        P("head", None),
        P("head"),
        P("ctx", "head"),
    )
    out_specs = (
        P("ctx", "head"),
        P("ctx", "head"),
        P("ctx", "head"),
        P("ctx", "head"),
        P("ctx", "head"),
        P("head", "ctx"),
    )
    return jax.shard_map(local, mesh=mesh, in_specs=in_specs, out_specs=out_specs, check_vma=False)
```

```python
import functools
import math

import jax
import jax.numpy as jnp
from jax import lax
from jax.experimental import pallas as pl
from jax.experimental.pallas import tpu as pltpu
from jax.sharding import PartitionSpec as P

D = 5376
HEADS = 32
HEAD_DIM = 128
WINDOW = 1024
EPSILON = 1e-06
ROPE_BASE = 10000.0
MASKED = -1e30


F32 = jnp.float32
BF16 = jnp.bfloat16


def send(value, axis, target):
    count = lax.axis_size(axis)
    pairs = [(i, target(i)) for i in range(count) if 0 <= target(i) < count]
    return lax.ppermute(value, axis, pairs)


def flip(value, axis, bit):
    return send(value, axis, lambda i: i ^ bit)


def gather_relative(value):
    pieces = [value]
    for j in range(1, lax.axis_size("head")):
        low = j & -j
        pieces.append(flip(pieces[j ^ low], "head", low))
    return pieces


def natural(pieces, head):
    bit = 1
    while bit < len(pieces):
        swap = (head & bit) != 0
        pieces = [jnp.where(swap, pieces[q ^ bit], pieces[q]) for q in range(len(pieces))]
        bit *= 2
    return pieces


def reduce_relative(keep, out):
    received = flip(out, "head", 1)
    sums = [keep[k].astype(F32) + received[k].astype(F32) for k in range(keep.shape[0])]
    bit = 2
    while len(sums) > 1:
        moved = flip(jnp.stack(sums[1::2]).astype(BF16), "head", bit)
        sums = [s + moved[k].astype(F32) for k, s in enumerate(sums[0::2])]
        bit *= 2
    return sums[0]


def gather_context(value):
    count = lax.axis_size("ctx")
    own = [value]
    for _ in range(count // 2 - 1):
        own.append(send(own[-1], "ctx", lambda i: (i + 2) % count))
    return own, [flip(v, "ctx", 1) for v in own]


def exchange_sides(chunks, ctx, event):
    count = lax.axis_size("ctx")
    depth = count // 2
    column, row = ctx % 2, ctx // 2

    def chunk(s):
        return lax.dynamic_index_in_dim(chunks, (row + s) % depth, 0, keepdims=False)

    arrived = [chunk(0)]
    for s in range(1, depth):
        arrived.append(send(chunk(s), "ctx", lambda i, s=s: (i + 2 * s) % count))
    arrived = after(jnp.stack(arrived), event)
    width = arrived.shape[2] // 2
    first, second = arrived[:, :, :width], arrived[:, :, width:]
    mine = jnp.where(column == 0, first, second)
    other = flip(jnp.where(column == 0, second, first), "ctx", 1)
    return jnp.stack([mine, other])


def gather_sides(sides, head):
    rows = natural(gather_relative(sides), head)
    return [
        [jnp.concatenate([r[side, s] for r in rows], axis=0) for s in range(sides.shape[1])]
        for side in range(2)
    ]


def split_columns(rows, parts):
    width = rows.shape[1] // parts
    return jnp.stack([rows[:, q * width : (q + 1) * width] for q in range(parts)])


def params(**kw):
    return pltpu.CompilerParams(vmem_limit_bytes=60 * 1024 * 1024, **kw)


def whole(shape):
    return pl.BlockSpec(shape, lambda *_: (0,) * len(shape))


def cost(flops, nbytes, transcendentals=0):
    return pl.CostEstimate(flops=flops, bytes_accessed=nbytes, transcendentals=transcendentals)


def turned(values, cos2, sin2):
    return values * cos2 + pltpu.roll(values, HEAD_DIM // 2, 1) * sin2


def project_kernel(count, heads, last, head_ref, *refs):
    pieces, refs = refs[:count], refs[count:]
    weights, refs = refs[: len(heads)], refs[len(heads) :]
    cos_ref, sin_ref, refs = refs[0], refs[1], refs[2:]
    starts, refs = (refs[: len(heads)], refs[len(heads) :]) if last else (None, refs)
    outs, totals = refs[: len(heads)], refs[len(heads) :]
    step = pl.program_id(0)
    for k, piece in enumerate(pieces):

        @pl.when(step == k)
        def _(k=k, piece=piece):
            for n, weight in enumerate(weights):
                term = jnp.dot(piece[...], weight[...], preferred_element_type=F32)
                if k == 0 and starts is not None:
                    term = term + starts[n][...]
                if k > 0:
                    term = term + totals[n][...]
                if k < count - 1:
                    totals[n][...] = term
                elif not last:
                    outs[n][...] = term
                elif heads[n]:
                    for c in range(term.shape[1] // HEAD_DIM):
                        cols = slice(c * HEAD_DIM, (c + 1) * HEAD_DIM)
                        outs[n][:, cols] = turned(
                            term[:, cols], cos_ref[...], sin_ref[...]
                        ).astype(BF16)
                else:
                    outs[n][...] = term.astype(BF16)


def project(head, base, pieces, weights, heads, cos2, sin2, starts, name):
    rows, depth = pieces[0].shape
    last = starts is not None
    count = len(pieces)
    in_specs = [whole((rows, depth))] * count
    in_specs += [pl.BlockSpec((depth, w.shape[1]), lambda i, h: (h[0] ^ (base + i), 0)) for w in weights]
    in_specs += [whole((rows, HEAD_DIM))] * 2
    if last:
        in_specs += [whole((rows, w.shape[1])) for w in weights]
    grid_spec = pltpu.PrefetchScalarGridSpec(
        num_scalar_prefetch=1,
        grid=(count,),
        in_specs=in_specs,
        out_specs=[whole((rows, w.shape[1])) for w in weights],
        scratch_shapes=[pltpu.VMEM((rows, w.shape[1]), F32) for w in weights],
    )
    size = sum(w.shape[1] for w in weights) * depth * count
    return pl.pallas_call(
        functools.partial(project_kernel, count, heads, last),
        grid_spec=grid_spec,
        out_shape=[
            jax.ShapeDtypeStruct((rows, w.shape[1]), BF16 if last else F32) for w in weights
        ],
        compiler_params=params(),
        cost_estimate=cost(2 * rows * size, 2 * size),
        name=name,
    )(head, *pieces, *weights, cos2, sin2, *(starts or ()))


def fill_bias(bias_ref, ctx, pos_ref):
    spans, rows, _ = bias_ref.shape
    for d in range(spans):
        key = lax.broadcasted_iota(jnp.int32, (rows, rows), 0)
        query = lax.broadcasted_iota(jnp.int32, (rows, rows), 1)
        distance = d * rows + query - key
        reach = jnp.where(ctx >= d, pos_ref[...], -1)
        allowed = (distance >= 0) & (distance < WINDOW) & (distance <= reach)
        bias_ref[d] = jnp.where(allowed, 0.0, MASKED)


def head_rows(ref, group):
    return jnp.concatenate(
        [ref[:, g * HEAD_DIM : (g + 1) * HEAD_DIM] for g in range(group)], axis=0
    )


def dot_on(left, right, left_dim, right_dim):
    return lax.dot_general(
        left, right, (((left_dim,), (right_dim,)), ((), ())), preferred_element_type=F32
    )


def forward_kernel(spans, group, scale, ctx_ref, pos_ref, q_ref, *refs):
    keys, values = refs[:spans], refs[spans : 2 * spans]
    out_ref, lse_ref, bias_ref, score_ref = refs[2 * spans :]

    @pl.when(pl.program_id(0) == 0)
    def _():
        fill_bias(bias_ref, ctx_ref[0], pos_ref)

    queries = head_rows(q_ref, group)
    highest = None
    for d in range(spans):
        scores = dot_on(keys[d][...], queries, 1, 1) * scale
        scores = scores + jnp.concatenate([bias_ref[d]] * group, axis=1)
        score_ref[d] = scores
        top = jnp.max(scores, axis=0, keepdims=True)
        highest = top if highest is None else jnp.maximum(highest, top)
    total = None
    for d in range(spans):
        exponent = jnp.exp(score_ref[d] - highest)
        score_ref[d] = exponent
        part = jnp.sum(exponent, axis=0, keepdims=True)
        total = part if total is None else total + part
    inverse = 1.0 / total
    mixed = None
    for d in range(spans):
        weights = (score_ref[d] * inverse).astype(BF16)
        part = dot_on(values[d][...], weights, 0, 0)
        mixed = part if mixed is None else mixed + part
    rows = mixed.T
    count = q_ref.shape[0]
    for g in range(group):
        out_ref[:, g * HEAD_DIM : (g + 1) * HEAD_DIM] = rows[
            g * count : (g + 1) * count
        ].astype(BF16)
    lse_ref[0] = highest + jnp.log(total)


def attend_forward(ctx, positions, queries, keys, values, group, scale):
    rows, cols = queries.shape
    spans = len(keys)
    kv = cols // (group * HEAD_DIM)
    wide = group * HEAD_DIM
    grid_spec = pltpu.PrefetchScalarGridSpec(
        num_scalar_prefetch=1,
        grid=(kv,),
        in_specs=[whole((1, rows)), pl.BlockSpec((rows, wide), lambda g, c: (0, g))]
        + [pl.BlockSpec((rows, HEAD_DIM), lambda g, c: (0, g))] * (2 * spans),
        out_specs=[
            pl.BlockSpec((rows, wide), lambda g, c: (0, g)),
            pl.BlockSpec((1, 1, group * rows), lambda g, c: (g, 0, 0)),
        ],
        scratch_shapes=[
            pltpu.VMEM((spans, rows, rows), F32),
            pltpu.VMEM((spans, rows, group * rows), F32),
        ],
    )
    area = spans * rows * rows * kv * group
    return pl.pallas_call(
        functools.partial(forward_kernel, spans, group, scale),
        grid_spec=grid_spec,
        out_shape=[
            jax.ShapeDtypeStruct((rows, cols), BF16),
            jax.ShapeDtypeStruct((kv, 1, group * rows), F32),
        ],
        compiler_params=params(),
        cost_estimate=cost(4 * area * HEAD_DIM, 8 * rows * cols, area),
        name="attend_forward",
    )(ctx, positions, queries, *keys, *values)


def backward_kernel(spans, group, scale, ctx_ref, pos_ref, q_ref, g_ref, lse_ref, *refs):
    cos_ref, sin_ref = refs[:2]
    keys, values = refs[2 : 2 + spans], refs[2 + spans : 2 + 2 * spans]
    dq_ref, refs = refs[2 + 2 * spans], refs[3 + 2 * spans :]
    dks, dvs = refs[:spans], refs[spans : 2 * spans]
    bias_ref, prob_ref, slope_ref = refs[2 * spans :]

    @pl.when(pl.program_id(0) == 0)
    def _():
        fill_bias(bias_ref, ctx_ref[0], pos_ref)

    queries = head_rows(q_ref, group)
    grads = head_rows(g_ref, group)
    lse = lse_ref[0]
    inner = None
    for d in range(spans):
        scores = dot_on(keys[d][...], queries, 1, 1) * scale
        scores = scores + jnp.concatenate([bias_ref[d]] * group, axis=1)
        probability = jnp.exp(scores - lse)
        slope = dot_on(values[d][...], grads, 1, 1)
        prob_ref[d] = probability
        slope_ref[d] = slope
        part = jnp.sum(probability * slope, axis=0, keepdims=True)
        inner = part if inner is None else inner + part
    total = None
    for d in range(spans):
        probability = prob_ref[d]
        dvs[d][...] = jnp.dot(
            probability.astype(BF16), grads, preferred_element_type=F32
        ).astype(dvs[d].dtype)
        change = (probability * (slope_ref[d] - inner)).astype(BF16)
        dks[d][...] = (jnp.dot(change, queries, preferred_element_type=F32) * scale).astype(
            dks[d].dtype
        )
        part = dot_on(keys[d][...], change, 0, 0)
        total = part if total is None else total + part
    rows = (total * scale).T
    count = q_ref.shape[0]
    for g in range(group):
        dq_ref[:, g * HEAD_DIM : (g + 1) * HEAD_DIM] = turned(
            rows[g * count : (g + 1) * count], cos_ref[...], -sin_ref[...]
        ).astype(BF16)


def attend_backward(ctx, positions, queries, grads, lse, cos2, sin2, keys, values, group, scale):
    rows, cols = queries.shape
    spans = len(keys)
    kv = cols // (group * HEAD_DIM)
    wide = group * HEAD_DIM
    pair_spec = pl.BlockSpec((rows, HEAD_DIM), lambda g, c: (0, g))
    row_spec = pl.BlockSpec((rows, wide), lambda g, c: (0, g))
    grid_spec = pltpu.PrefetchScalarGridSpec(
        num_scalar_prefetch=1,
        grid=(kv,),
        in_specs=[
            whole((1, rows)),
            row_spec,
            row_spec,
            pl.BlockSpec((1, 1, group * rows), lambda g, c: (g, 0, 0)),
            whole((rows, HEAD_DIM)),
            whole((rows, HEAD_DIM)),
        ]
        + [pair_spec] * (2 * spans),
        out_specs=[row_spec] + [pair_spec] * (2 * spans),
        scratch_shapes=[
            pltpu.VMEM((spans, rows, rows), F32),
            pltpu.VMEM((spans, rows, group * rows), F32),
            pltpu.VMEM((spans, rows, group * rows), F32),
        ],
    )
    area = spans * rows * rows * kv * group
    shape = (rows, kv * HEAD_DIM)
    parts = [jax.ShapeDtypeStruct(shape, F32)]
    parts += [jax.ShapeDtypeStruct(shape, BF16)] * (spans - 1)
    return pl.pallas_call(
        functools.partial(backward_kernel, spans, group, scale),
        grid_spec=grid_spec,
        out_shape=[jax.ShapeDtypeStruct((rows, cols), BF16)] + parts + parts,
        compiler_params=params(),
        cost_estimate=cost(10 * area * HEAD_DIM, 16 * rows * cols, area),
        name="attend_backward",
    )(ctx, positions, queries, grads, lse, cos2, sin2, *keys, *values)


def branch_kernel(count, head_ref, a_ref, w_ref, keep_ref, out_ref):
    rows = a_ref.shape[0] // count
    order = list(range(0, count, 2)) + list(range(1, count, 2))
    left = jnp.concatenate(
        [a_ref[pl.ds(pl.multiple_of((head_ref[0] ^ j) * rows, 16), rows), :] for j in order],
        axis=0,
    )
    total = jnp.dot(left, w_ref[...], preferred_element_type=F32).astype(BF16)
    half = count // 2
    for k in range(half):
        keep_ref[k] = total[k * rows : (k + 1) * rows]
        out_ref[k] = total[(half + k) * rows : (half + k + 1) * rows]


def project_branch(head, attended, w_out, count, part, parts):
    rows, depth = attended.shape
    cols = w_out.shape[1] // parts
    block = cols // 3 if cols % 384 == 0 else 128
    steps = cols // block
    shape = jax.ShapeDtypeStruct((count // 2, rows // count, cols), BF16)
    spec = pl.BlockSpec((count // 2, rows // count, block), lambda i, h: (0, 0, i))
    grid_spec = pltpu.PrefetchScalarGridSpec(
        num_scalar_prefetch=1,
        grid=(steps,),
        in_specs=[
            whole((rows, depth)),
            pl.BlockSpec((depth, block), lambda i, h: (0, part * steps + i)),
        ],
        out_specs=[spec, spec],
    )
    return pl.pallas_call(
        functools.partial(branch_kernel, count),
        grid_spec=grid_spec,
        out_shape=[shape, shape],
        compiler_params=params(),
        cost_estimate=cost(2 * rows * depth * cols, 2 * depth * cols),
        name="project_branch",
    )(head, attended, w_out)


def attended_grad_kernel(count, last, head_ref, *refs):
    pieces, (w_ref, *starts, out_ref, rows_ref) = refs[:count], refs[count:]
    rows = pieces[0].shape[0]

    @pl.when(pl.program_id(0) == 0)
    def _():
        for j, piece in enumerate(pieces):
            start = pl.multiple_of((head_ref[0] ^ j) * rows, 16)
            rows_ref[pl.ds(start, rows), :] = piece[...]

    total = dot_on(rows_ref[...], w_ref[...], 1, 1)
    for start in starts:
        total = total + start[...]
    out_ref[...] = total.astype(out_ref.dtype)


def attended_grad(head, pieces, w_out, part, start, last):
    rows, cols = pieces[0].shape
    count = len(pieces)
    block = min(256, w_out.shape[0])
    tile = pl.BlockSpec((rows * count, block), lambda i, h: (0, i))
    grid_spec = pltpu.PrefetchScalarGridSpec(
        num_scalar_prefetch=1,
        grid=(w_out.shape[0] // block,),
        in_specs=[whole((rows, cols))] * count
        + [pl.BlockSpec((block, cols), lambda i, h: (i, part))]
        + ([] if start is None else [tile]),
        out_specs=tile,
        scratch_shapes=[pltpu.VMEM((rows * count, cols), BF16)],
    )
    size = w_out.shape[0] * cols
    return pl.pallas_call(
        functools.partial(attended_grad_kernel, count, last),
        grid_spec=grid_spec,
        out_shape=jax.ShapeDtypeStruct((rows * count, w_out.shape[0]), BF16 if last else F32),
        compiler_params=params(),
        cost_estimate=cost(2 * rows * count * size, 2 * size),
        name="attended_grad",
    )(head, *pieces, w_out, *([] if start is None else [start]))


def inputs_grad_kernel(head_ref, q_ref, k_ref, v_ref, wq_ref, wk_ref, wv_ref, out_ref):
    total = dot_on(wq_ref[...], q_ref[...], 1, 1)
    total = total + dot_on(wk_ref[...], k_ref[...], 1, 1)
    total = total + dot_on(wv_ref[...], v_ref[...], 1, 1)
    out_ref[0] = total.astype(BF16)


def inputs_grad(head, parity, count, dq, dk, dv, w_query, w_key, w_value):
    rows = dq.shape[0]
    depth = w_query.shape[0] // count

    def weight_spec(weight):
        return pl.BlockSpec((depth, weight.shape[1]), lambda i, h: (h[0] ^ (2 * i + parity), 0))

    grid_spec = pltpu.PrefetchScalarGridSpec(
        num_scalar_prefetch=1,
        grid=(count // 2,),
        in_specs=[whole(dq.shape), whole(dk.shape), whole(dv.shape)]
        + [weight_spec(w) for w in (w_query, w_key, w_value)],
        out_specs=pl.BlockSpec((1, depth, rows), lambda i, h: (i, 0, 0)),
    )
    size = (w_query.size + 2 * w_key.size) // 2
    return pl.pallas_call(
        inputs_grad_kernel,
        grid_spec=grid_spec,
        out_shape=jax.ShapeDtypeStruct((count // 2, depth, rows), BF16),
        compiler_params=params(),
        cost_estimate=cost(2 * rows * size, 2 * size),
        name="inputs_grad",
    )(head, dq, dk, dv, w_query, w_key, w_value)


def weight_grad_kernel(count, *refs):
    lefts, rights, (*starts, out_ref) = refs[:count], refs[count : 2 * count], refs[2 * count :]
    total = None
    for left, right in zip(lefts, rights, strict=True):
        term = dot_on(left[...], right[...], 0, 0)
        total = term if total is None else total + term
    for start in starts:
        total = total + start[...]
    out_ref[...] = total


def weight_grad(lefts, rights, start):
    rows, height = lefts[0].shape
    width = rights[0].shape[1]
    block = min(512, width)
    count = len(lefts)
    tile = pl.BlockSpec((height, block), lambda i: (0, i))
    size = rows * count
    starts = [] if start is None else [start]
    return pl.pallas_call(
        functools.partial(weight_grad_kernel, count),
        grid=(width // block,),
        in_specs=[whole((rows, height))] * count
        + [pl.BlockSpec((rows, block), lambda i: (0, i))] * count
        + [tile] * len(starts),
        out_specs=tile,
        out_shape=jax.ShapeDtypeStruct((height, width), F32),
        input_output_aliases={2 * count: 0} if starts else {},
        compiler_params=params(),
        cost_estimate=cost(
            2 * size * height * width, 2 * size * (height + width) + 8 * height * width
        ),
        name="weight_grad",
    )(*lefts, *rights, *starts)


def paired(both, first, last):
    return [v for s in range(first, last) for v in (both[0][s], both[1][s])]


def grow_weight_grad(lefts, rights, cuts):
    total = None
    for first, last in zip(cuts, cuts[1:]):
        total = weight_grad(paired(lefts, first, last), paired(rights, first, last), total)
    return total


def after(value, *events):
    return lax.optimization_barrier((value, *events))[0]


def local(inputs, positions, w_query, w_key, w_value, w_out, post_gain, cotangent):
    tok_rows, part_cols = inputs.shape
    n_ctx, n_head = lax.axis_size("ctx"), lax.axis_size("head")
    kv_cols = w_key.shape[1]
    group = w_query.shape[1] // kv_cols
    halo = WINDOW // tok_rows
    steps = halo // 2
    depth = n_ctx // 2
    own_rows = tok_rows // n_head
    scale = (D // HEADS) ** (-0.5)
    ctx, head = lax.axis_index("ctx"), lax.axis_index("head")
    ctx_arg, head_arg = ctx.reshape(1), head.reshape(1)
    column = ctx % 2
    half = HEAD_DIM // 2
    frequency = jnp.exp(jnp.arange(half, dtype=F32) * (-2.0 * math.log(ROPE_BASE) / HEAD_DIM))
    angles = positions.astype(F32)[:, None] * frequency[None, :]
    cosine, sine = jnp.cos(angles), jnp.sin(angles)
    cos2 = jnp.concatenate([cosine, cosine], axis=1)
    sin2 = jnp.concatenate([-sine, sine], axis=1)
    pos_row = positions.reshape(1, tok_rows)

    pieces = gather_relative(inputs)
    near, far = pieces[:2], pieces[2:]
    start_k, start_v = project(
        head_arg, 0, near, [w_key, w_value], [True, False], cos2, sin2, None, "project_pair"
    )
    (start_q,) = project(head_arg, 0, near, [w_query], [True], cos2, sin2, None, "project_query")
    far = list(lax.optimization_barrier((*far, start_k, start_q))[: len(far)])
    key, value = project(
        head_arg, 2, far, [w_key, w_value], [True, False], cos2, sin2,
        [start_k, start_v], "project_pair",
    )

    def halo_of(mine):
        chain, crossed = [mine], []
        for i in range(steps):
            chain.append(send(chain[-1], "ctx", lambda i: i + 2))
            crossed.append(flip(jnp.where(column == 0, chain[i], chain[i + 1]), "ctx", 1))
        spans = [mine]
        for i in range(steps):
            spans += [crossed[i], chain[i + 1]]
        return spans

    keys, values = halo_of(key), halo_of(value)
    (queries,) = project(
        head_arg, 2, [after(far[0], key)] + far[1:], [w_query], [True], cos2, sin2, [start_q], "project_query"
    )

    late_cotangent = after(cotangent, key)
    bundles = []
    for j in range(n_head):
        rows = lax.dynamic_slice_in_dim(late_cotangent, (head ^ j) * own_rows, own_rows, 0)
        bundle = jnp.concatenate([rows, post_gain[None, :]], axis=0)
        bundles.append(flip(bundle, "head", j) if j else bundle)
    input_parts = natural(
        [
            lax.dynamic_slice_in_dim(p, head * own_rows, own_rows, 0)
            for p in near + far
        ],
        head,
    )
    bundle_rows = jnp.concatenate(natural(bundles, head), axis=1).astype(F32)
    input_rows = jnp.concatenate(input_parts, axis=1)
    bundle_rows, input_rows = lax.optimization_barrier((bundle_rows, input_rows))
    cotangent_rows, gain = bundle_rows[:own_rows], bundle_rows[own_rows:]
    input_chunks = (
        jnp.stack(input_parts) if depth == n_head else split_columns(input_rows, depth)
    )
    input_sides = exchange_sides(after(input_chunks, keys[-1]), ctx, queries)

    ready = lax.optimization_barrier((queries, bundle_rows, input_rows))[0]
    attended, lse = attend_forward(ctx_arg, pos_row, ready, keys, values, group, scale)

    parts = 2
    branches = []
    for part in range(parts):
        keep, out = project_branch(head_arg, attended, w_out, n_head, part, parts)
        branches.append(reduce_relative(keep, out))
    branch = jnp.concatenate(branches, axis=1)
    inverse_norm = lax.rsqrt(jnp.sum(branch * branch, axis=1, keepdims=True) / D + EPSILON)
    normed = branch * inverse_norm
    scaled_grad = cotangent_rows * gain
    slopes = jnp.sum(scaled_grad * normed, axis=1, keepdims=True)
    branch_grad = (inverse_norm * (scaled_grad - normed * (slopes / D))).astype(BF16)
    grad_attended = None
    for part in range(parts):
        width = D // parts
        gathered = gather_relative(branch_grad[:, part * width : (part + 1) * width])
        grad_attended = attended_grad(
            head_arg, gathered, w_out, part, grad_attended, part == parts - 1
        )
    late_branch, late_normed = lax.optimization_barrier((branch_grad, normed, grad_attended))[:2]
    hidden_rows = (input_rows.astype(F32) + late_normed * gain).astype(BF16)

    attended_all = gather_context(attended)
    input_cols = gather_sides(after(input_sides, grad_attended), head)

    grads = attend_backward(
        ctx_arg, pos_row, queries, grad_attended, lse, cos2, sin2, keys, values, group, scale
    )
    grad_query_rows = grads[0]

    def halo_sum(parts):
        crossing = {d: flip(parts[d], "ctx", 1) for d in range(halo - 1, 0, -2)}
        carried = None
        for i in range(steps, -1, -1):
            slot = parts[2 * i].astype(F32)
            here = crossing[2 * i + 1].astype(F32) if i < steps else 0.0
            there = crossing[2 * i - 1].astype(F32) if i > 0 else 0.0
            slot = slot + jnp.where(column == 0, here, there)
            if carried is not None:
                slot = slot + carried.astype(F32)
            if i > 0:
                carried = send(slot.astype(BF16), "ctx", lambda i: i - 2)
        return slot

    key_sum = halo_sum(grads[1 : 2 + halo])
    value_sum = halo_sum(grads[2 + halo :])
    key_heads = key_sum.reshape(tok_rows, kv_cols // HEAD_DIM, HEAD_DIM)
    swapped = jnp.concatenate([key_heads[..., half:], key_heads[..., :half]], axis=-1)
    grad_key_rows = key_heads * cos2[:, None, :] - swapped * sin2[:, None, :]
    grad_key_rows = grad_key_rows.reshape(tok_rows, kv_cols).astype(BF16)
    grad_value_rows = value_sum.astype(BF16)

    query_all = gather_context(grad_query_rows)
    key_all = gather_context(grad_key_rows)
    value_all = gather_context(grad_value_rows)
    grad_sides = exchange_sides(split_columns(branch_grad, depth), ctx, grad_attended)
    grad_cols = gather_sides(after(grad_sides, grad_query_rows), head)
    grad_w_out_t = grow_weight_grad(grad_cols, attended_all, [0, depth])

    late = lax.optimization_barrier((grad_query_rows, grad_key_rows, grad_value_rows))
    moved = [
        inputs_grad(head_arg, parity, n_head, *late, w_query, w_key, w_value)
        for parity in (1, 0)
    ]
    grad_inputs_t = (
        cotangent.T.astype(F32) + reduce_relative(moved[1], moved[0])
    ).astype(BF16)
    cuts = [0, (depth + 1) // 2, depth]
    grad_w_query = grow_weight_grad(input_cols, query_all, cuts)
    fine = [0, (depth + 1) // 2, depth - 1, depth]
    grad_w_key = grow_weight_grad(input_cols, key_all, fine)
    grad_w_value = grow_weight_grad(input_cols, value_all, fine)

    hidden_chunks = split_columns(after(hidden_rows, grad_query_rows), n_head)
    hidden_parts = []
    for j in range(n_head):
        chunk = lax.dynamic_index_in_dim(hidden_chunks, head ^ j, 0, keepdims=False)
        hidden_parts.append(flip(chunk, "head", j) if j else chunk)
    hidden = jnp.concatenate(natural(hidden_parts, head), axis=0)
    return (
        hidden,
        grad_inputs_t.T,
        grad_w_query,
        grad_w_key,
        grad_w_value,
        grad_w_out_t.T,
    )


def solution(mesh):
    in_specs = (
        P("ctx", "head"),
        P("ctx"),
        P(None, "head"),
        P(None, "head"),
        P(None, "head"),
        P("head", None),
        P("head"),
        P("ctx", "head"),
    )
    out_specs = (
        P("ctx", "head"),
        P("ctx", "head"),
        P("ctx", "head"),
        P("ctx", "head"),
        P("ctx", "head"),
        P("head", "ctx"),
    )
    return jax.shard_map(local, mesh=mesh, in_specs=in_specs, out_specs=out_specs, check_vma=False)
```
